32 devices in a mesh: tgt: 4 (over y, core), blk: 8 (over z, x).
Axes of the slice: x: 2, y: 2, z: 4, core: 2. Of those that a mesh axis runs over, the one named last changes fastest.
Arguments:
- integrals: bfloat16 [8192, 128, 128], P(('tgt', 'blk')), may hold values from -0.5 to 0.5
- densities: bfloat16 [60, 128, 128], P('tgt'), may hold values from -1.5 to 1.5
- entry_block: int32 [65536], P(('tgt', 'blk')), may hold values from 0 to 255
- entry_state: int32 [65536], P(('tgt', 'blk')), may hold values from 0 to 59, as said below
- entry_slot: int32 [65536], P(('tgt', 'blk')), may hold values from 0 to 127
- counts: int32 [32, 4], P(('tgt', 'blk')), may hold values from 0 to 2048, as said below
- owner: int32 [1024], P('blk'), may hold values from 0 to 1023, as said below
Outputs:
- hamiltonian: float32 [1024, 128, 128], P(('tgt', 'blk'))
The draws below stay inside these ranges and needn't reach their ends.
Inputs may be any that keep to these rules, and one draw needn't show every extreme that they name: `counts`: each row sums to at most 2048; on some device all 2048 slots are live and belong to a single group of target states. `entry_state`: within each device's slots, the first counts[d, 0] name states of group 0 (states 0 to 14), the next counts[d, 1] states of group 1, and so on; the slots after the live ones are unused. `owner`: A permutation of 0 to 1023; output positions d * 32 to (d + 1) * 32 - 1 belong to device d, and of the 128 blocks of one block-row group exactly 4 go to each device.
All inputs are finite; a program needn't handle non-finite values.
Results may differ from the reference program's by a relative error of at most 0.0003.
Values may be sent and summed in bfloat16 or wider, within the bound.
A program may use at most 128 MiB of HBM per device.

```python
import jax
import jax.numpy as jnp
from jax import lax

BS = 128
STATES = 60
E_CAP = 2048
G_DEV = 256
HB_DEV = 128
SHARDS = 4
BLOCK_GROUPS = 8
S_DEV = 15
NH = 1024
OWN_DEV = 32
PER_DEV = 4
N_BLK = 8
DEVICES = 32


def segment_counts(key):
    ndev = SHARDS * BLOCK_GROUPS
    key_a, key_b, key_c, key_d, key_e = jax.random.split(key, 5)
    totals = jax.random.randint(key_a, (ndev,), E_CAP // 8, E_CAP // 2 + 1)
    packed = jax.random.randint(key_b, (ndev,), 0, 8) == 0
    forced = jnp.arange(ndev) == jax.random.randint(key_c, (), 0, ndev)
    totals = jnp.where(packed | forced, E_CAP, totals).astype(jnp.int32)
    cuts = jnp.sort(jax.random.randint(key_d, (ndev, SHARDS - 1), 0, E_CAP + 1), axis=1)
    chosen = jax.random.randint(key_e, (), 0, SHARDS)
    single = jnp.where(jnp.arange(SHARDS - 1) < chosen, 0, E_CAP).astype(jnp.int32)
    cuts = jnp.where(forced[:, None], single[None, :], cuts)
    cuts = cuts * totals[:, None] // E_CAP
    edges = jnp.concatenate([jnp.zeros((ndev, 1), jnp.int32), cuts.astype(jnp.int32), totals[:, None]], axis=1)
    return jnp.diff(edges, axis=1).astype(jnp.int32)


def draw_counts(key, part):
    return segment_counts(jax.random.fold_in(key, 11))


def draw_entry_state(key, part):
    counts = segment_counts(jax.random.fold_in(key, 11))
    ndev = SHARDS * BLOCK_GROUPS
    ends = jnp.cumsum(counts, axis=1)
    pos = jnp.arange(E_CAP, dtype=jnp.int32)
    group = jnp.sum((pos[None, :, None] >= ends[:, None, :SHARDS - 1]).astype(jnp.int32), axis=2)
    live = pos[None, :] < ends[:, -1:]
    key_a, key_b = jax.random.split(jax.random.fold_in(key, 23))
    spare = jax.random.randint(key_a, (ndev, E_CAP), 0, SHARDS)
    group = jnp.where(live, group, spare)
    inner = jax.random.randint(key_b, (ndev, E_CAP), 0, S_DEV)
    return (group * S_DEV + inner).astype(jnp.int32).reshape(-1)


def draw_owner(key, part):
    key_a, key_b = jax.random.split(jax.random.fold_in(key, 37))
    ndev = SHARDS * BLOCK_GROUPS
    source_keys = jax.random.split(key_a, BLOCK_GROUPS)
    dest = jax.vmap(lambda k: jax.random.permutation(k, HB_DEV))(source_keys).astype(jnp.int32)
    device = dest // PER_DEV
    within = dest % PER_DEV
    before = jnp.arange(BLOCK_GROUPS, dtype=jnp.int32)[:, None] * PER_DEV + within
    device_keys = jax.random.split(key_b, ndev)
    shuffle = jax.vmap(lambda k: jax.random.permutation(k, OWN_DEV))(device_keys).astype(jnp.int32)
    local = shuffle[device, before]
    return (device * OWN_DEV + local).astype(jnp.int32).reshape(-1)


def plant(array, key, smallest, high):
    shape = array.shape
    index_at = [jax.random.randint(jax.random.fold_in(key, axis), (), 0, shape[axis]) for axis in range(len(shape))]
    array = array.at[tuple(index_at)].set(smallest)
    longest = shape.index(max(shape))
    index_at[longest] = (index_at[longest] + 1) % shape[longest]
    return array.at[tuple(index_at)].set(high)


def levels(own_key, extent, shards, low, top_value):
    loudness, own = 1.0, jax.random.fold_in(own_key, 6)
    for dim, shards_of in shards:
        heights = jnp.exp(jax.random.uniform(jax.random.fold_in(own, dim), (shards_of,), jnp.float32, low / len(shards), top_value / len(shards)))
        loudness = loudness * jnp.repeat(heights, extent[dim] // shards_of).reshape([-1 if axis == dim else 1 for axis in range(len(extent))])
    return loudness


def noise(key, dims, scale, limit, pieces=(), held_as=jnp.bfloat16):
    array = scale * jax.random.normal(key, dims, jnp.float32)
    if pieces:
        array = array * levels(key, dims, pieces, -0.22, 0.18)
    return jnp.clip(array, -limit, limit).astype(held_as)


def setup_inputs(seed: int = 0) -> dict:
    keys = jax.random.split(jax.random.key(seed), 8)
    integrals = noise(keys[0], (DEVICES * G_DEV, BS, BS), BS ** -0.5, 0.5, ((0, 32),))
    densities = noise(keys[1], (STATES, BS, BS), 0.25, 1.5, ((0, 4),))
    entry_block = plant(jax.random.randint(keys[2], (DEVICES * E_CAP,), 0, G_DEV), jax.random.fold_in(keys[2], 1), 0, G_DEV - 1).astype(jnp.int32)
    entry_state = draw_entry_state(jax.random.fold_in(keys[7], 71), 0)
    entry_slot = plant(jax.random.randint(keys[4], (DEVICES * E_CAP,), 0, HB_DEV), jax.random.fold_in(keys[4], 1), 0, HB_DEV - 1).astype(jnp.int32)
    counts = draw_counts(jax.random.fold_in(keys[7], 71), 0)
    owner = draw_owner(jax.random.fold_in(keys[7], 71), 0)
    return {"integrals": integrals, "densities": densities, "entry_block": entry_block, "entry_state": entry_state, "entry_slot": entry_slot, "counts": counts, "owner": owner}


def reference(integrals, densities, entry_block, entry_state, entry_slot, counts, owner):
    devices = counts.shape[0]
    width = min(128, E_CAP)
    blocks = entry_block.reshape(devices, E_CAP)
    states = entry_state.reshape(devices, E_CAP)
    slots = entry_slot.reshape(devices, E_CAP)
    totals = jnp.sum(counts, axis=1).astype(jnp.int32)
    flat = BS * BS

    def per_device(full, dev):
        local = lax.dynamic_slice_in_dim(integrals, (dev * G_DEV).astype(jnp.int32), G_DEV, 0)
        live_total = totals[dev]
        steps = (live_total + width - 1) // width

        def group(j, acc):
            begin = (j * width).astype(jnp.int32)
            pos = begin + jnp.arange(width, dtype=jnp.int32)
            valid = pos < live_total
            blk_ids = lax.dynamic_slice_in_dim(blocks[dev], begin, width)
            st_ids = lax.dynamic_slice_in_dim(states[dev], begin, width)
            sl_ids = lax.dynamic_slice_in_dim(slots[dev], begin, width)
            left = local[blk_ids].astype(jnp.float32)
            right = densities[st_ids].astype(jnp.float32)
            prod = jnp.einsum("ekm,emn->ekn", left, right)
            prod = jnp.where(valid[:, None, None], prod, jnp.zeros_like(prod))
            return acc.at[sl_ids].add(prod.reshape(width, flat))

        partial_value = lax.fori_loop(0, steps, group, jnp.zeros((HB_DEV, flat), jnp.float32))
        row = ((dev % N_BLK) * HB_DEV).astype(jnp.int32)
        current = lax.dynamic_slice_in_dim(full, row, HB_DEV, 0)
        full = lax.dynamic_update_slice_in_dim(full, current + partial_value, row, 0)
        return full, None

    full, _ = lax.scan(per_device, jnp.zeros((NH, flat), jnp.float32), jnp.arange(devices, dtype=jnp.int32))
    placed = jnp.zeros_like(full).at[owner].set(full)
    return placed.reshape(NH, BS, BS)
```

```python
import jax
import jax.numpy as jnp
from jax import lax
from jax.experimental import pallas as pl
from jax.experimental.pallas import tpu as pltpu
from jax.sharding import PartitionSpec as P

CHUNK = 4
UNROLL = 2


def bits_for(n):
    return max(1, (n - 1).bit_length())


def accumulate(n_steps, keys, place, integrals, densities, st_bits, blk_bits, hb_rows):
    states, size, _ = densities.shape
    held = integrals.shape[0]
    st_mask = (1 << st_bits) - 1
    blk_mask = (1 << blk_bits) - 1

    def kernel(n_ref, keys_ref, place_ref, int_hbm, den_hbm, out_hbm, ints, dens, acc, sems):
        load_ints = pltpu.make_async_copy(int_hbm, ints, sems.at[0])
        load_dens = pltpu.make_async_copy(den_hbm, dens.at[pl.ds(0, states)], sems.at[1])
        load_ints.start()
        load_dens.start()
        dens[states] = jnp.zeros((size, size), dens.dtype)

        @pl.loop(0, hb_rows)
        def _(j):
            acc[j] = jnp.zeros((size, size), jnp.float32)

        load_ints.wait()
        load_dens.wait()

        @pl.loop(0, n_ref[0])
        def _(step):
            prods = []
            for u in range(UNROLL):
                base = (step * UNROLL + u) * CHUNK
                ks = [keys_ref[base + i] for i in range(CHUNK)]
                lhs = jnp.concatenate([ints[(k >> st_bits) & blk_mask] for k in ks], axis=1)
                rhs = jnp.concatenate([dens[k & st_mask] for k in ks], axis=0)
                row = place_ref[ks[0] >> (st_bits + blk_bits)]
                prods.append((row, jnp.dot(lhs, rhs, preferred_element_type=jnp.float32)))
            for row, prod in prods:
                acc[row] += prod

        store = pltpu.make_async_copy(acc, out_hbm, sems.at[2])
        store.start()
        store.wait()

    smem = pl.BlockSpec(memory_space=pltpu.SMEM)
    hbm = pl.BlockSpec(memory_space=pl.ANY)
    return pl.pallas_call(
        kernel,
        out_shape=jax.ShapeDtypeStruct((hb_rows, size, size), jnp.float32),
        in_specs=[smem, smem, smem, hbm, hbm],
        out_specs=hbm,
        scratch_shapes=[
            pltpu.VMEM((held, size, size), integrals.dtype),
            pltpu.VMEM((states + 1, size, size), densities.dtype),
            pltpu.VMEM((hb_rows, size, size), jnp.float32),
            pltpu.SemaphoreType.DMA((3,)),
        ],
        compiler_params=pltpu.CompilerParams(vmem_limit_bytes=40 << 20),
    )(n_steps, keys, place, integrals, densities)


def make_keys(entry_block, entry_state, entry_slot, live, hb_rows, held, states):
    st_bits = bits_for(states + 1)
    blk_bits = bits_for(held)
    e_cap = entry_block.shape[0]
    valid = jnp.arange(e_cap, dtype=jnp.int32) < live
    slots = jnp.arange(hb_rows, dtype=jnp.int32)
    per_slot = jnp.sum(
        ((entry_slot[:, None] == slots[None, :]) & valid[:, None]).astype(jnp.int32), axis=0
    )
    spare = (-per_slot) % CHUNK
    filler = (slots << (st_bits + blk_bits)) + ((held - 1) << st_bits) + states
    last = filler[hb_rows - 1]
    key = (((entry_slot << blk_bits) + entry_block) << st_bits) + entry_state
    key = jnp.where(valid, key, last)
    order = jnp.arange(CHUNK - 1, dtype=jnp.int32)
    fill = jnp.where(order[:, None] < spare[None, :], filler[None, :], last).reshape(-1)
    total = e_cap + fill.shape[0]
    group = CHUNK * UNROLL
    tail = jnp.full(((-total) % group,), last, jnp.int32)
    keys = lax.sort(jnp.concatenate([key, fill, tail]))
    n_steps = (jnp.sum(per_slot + spare) + group - 1) // group
    return keys, n_steps.reshape(1), st_bits, blk_bits


def on_device(integrals, densities, entry_block, entry_state, entry_slot, counts, owner):
    size = integrals.shape[1]
    hb_rows = owner.shape[0]
    n_tgt = lax.axis_size("tgt")
    n_blk = lax.axis_size("blk")
    own_rows = hb_rows // n_tgt
    piece = lax.all_gather(densities, "tgt", axis=0, tiled=True)
    keys, n_steps, st_bits, blk_bits = make_keys(
        entry_block, entry_state, entry_slot, jnp.sum(counts[0]), hb_rows,
        integrals.shape[0], piece.shape[0],
    )
    place = jnp.sum((owner[None, :] < owner[:, None]).astype(jnp.int32), axis=1)
    partial = accumulate(n_steps, keys, place, integrals, piece, st_bits, blk_bits, hb_rows)
    mine = lax.psum_scatter(partial, "tgt", scatter_dimension=0, tiled=True)
    sorted_owner = lax.sort(owner)
    pos = lax.dynamic_slice_in_dim(sorted_owner, lax.axis_index("tgt") * own_rows, own_rows)
    got = lax.all_to_all(mine, "blk", split_axis=0, concat_axis=0, tiled=True)
    got_pos = lax.all_to_all(pos, "blk", split_axis=0, concat_axis=0, tiled=True)
    return got[jnp.argsort(got_pos)]


def solution(mesh):
    in_specs = (
        P(("tgt", "blk"), None, None),
        P("tgt", None, None),
        P(("tgt", "blk")),
        P(("tgt", "blk")),
        P(("tgt", "blk")),
        P(("tgt", "blk"), None),
        P("blk"),
    )
    out_specs = P(("tgt", "blk"), None, None)
    return jax.shard_map(
        on_device, mesh=mesh, in_specs=in_specs, out_specs=out_specs, check_vma=False
    )
```

```python
import jax
import jax.numpy as jnp
from jax import lax
from jax.experimental import pallas as pl
from jax.experimental.pallas import tpu as pltpu
from jax.sharding import PartitionSpec as P

CHUNK = 4
UNROLL = 2
STEPS = 8
LAG = 1
MESH = pl.DeviceIdType.MESH


def bits_for(n):
    return max(1, (n - 1).bit_length())


def accumulate(n_steps, keys, place, integrals, densities, st_bits, blk_bits, hb_rows):
    states, size, _ = densities.shape
    held = integrals.shape[0]
    st_mask = (1 << st_bits) - 1
    blk_mask = (1 << blk_bits) - 1

    def kernel(n_ref, keys_ref, place_ref, int_hbm, den_hbm, acc, ints, dens, sems):
        load_ints = pltpu.make_async_copy(int_hbm, ints, sems.at[0])
        load_dens = pltpu.make_async_copy(den_hbm, dens.at[pl.ds(0, states)], sems.at[1])
        load_ints.start()
        load_dens.start()
        dens[states] = jnp.zeros((size, size), dens.dtype)

        @pl.loop(0, hb_rows)
        def _(j):
            acc[j] = jnp.zeros((size, size), jnp.float32)

        load_ints.wait()
        load_dens.wait()

        @pl.loop(0, n_ref[0])
        def _(step):
            prods = []
            for u in range(UNROLL):
                base = (step * UNROLL + u) * CHUNK
                ks = [keys_ref[base + i] for i in range(CHUNK)]
                lhs = jnp.concatenate([ints[(k >> st_bits) & blk_mask] for k in ks], axis=1)
                rhs = jnp.concatenate([dens[k & st_mask] for k in ks], axis=0)
                row = place_ref[ks[0] >> (st_bits + blk_bits)]
                prods.append((row, jnp.dot(lhs, rhs, preferred_element_type=jnp.float32)))
            for row, prod in prods:
                acc[row] += prod

    smem = pl.BlockSpec(memory_space=pltpu.SMEM)
    hbm = pl.BlockSpec(memory_space=pl.ANY)
    return pl.pallas_call(
        kernel,
        out_shape=jax.ShapeDtypeStruct((hb_rows, size, size), jnp.float32),
        in_specs=[smem, smem, smem, hbm, hbm],
        out_specs=pl.BlockSpec(memory_space=pltpu.VMEM),
        scratch_shapes=[
            pltpu.VMEM((held, size, size), integrals.dtype),
            pltpu.VMEM((states + 1, size, size), densities.dtype),
            pltpu.SemaphoreType.DMA((2,)),
        ],
        compiler_params=pltpu.CompilerParams(vmem_limit_bytes=40 << 20),
    )(n_steps, keys, place, integrals, densities)


def make_keys(entry_block, entry_state, entry_slot, live, hb_rows, held, states):
    st_bits = bits_for(states + 1)
    blk_bits = bits_for(held)
    e_cap = entry_block.shape[0]
    valid = jnp.arange(e_cap, dtype=jnp.int32) < live
    slots = jnp.arange(hb_rows, dtype=jnp.int32)
    per_slot = jnp.sum(
        ((entry_slot[:, None] == slots[None, :]) & valid[:, None]).astype(jnp.int32), axis=0
    )
    spare = (-per_slot) % CHUNK
    filler = (slots << (st_bits + blk_bits)) + ((held - 1) << st_bits) + states
    last = filler[hb_rows - 1]
    key = (((entry_slot << blk_bits) + entry_block) << st_bits) + entry_state
    key = jnp.where(valid, key, last)
    order = jnp.arange(CHUNK - 1, dtype=jnp.int32)
    fill = jnp.where(order[:, None] < spare[None, :], filler[None, :], last).reshape(-1)
    total = e_cap + fill.shape[0]
    group = CHUNK * UNROLL
    tail = jnp.full(((-total) % group,), last, jnp.int32)
    keys = lax.sort(jnp.concatenate([key, fill, tail]))
    n_steps = (jnp.sum(per_slot + spare) + group - 1) // group
    return keys, n_steps.reshape(1), st_bits, blk_bits


def exchange(partial, pos, own_rows, n_blk):
    size = partial.shape[-1]
    steps = min(STEPS, n_blk)
    rows = own_rows // steps
    dests = n_blk // steps
    per = own_rows // n_blk

    def kernel(part, pos_ref, out, pos_out, r1, s2, r2, mine,
               s1_send, s1_recv, s2_send, s2_recv, s3_send, s3_recv, p_send, p_recv, own_sem):
        t = lax.axis_index("tgt")
        b = lax.axis_index("blk")
        y, c = t // 2, t % 2
        sibling = y * 2 + (1 - c)
        across = (1 - y) * 2 + c
        barrier = pltpu.get_barrier_semaphore()
        pl.semaphore_signal(barrier, inc=1, device_id={"tgt": sibling}, device_id_type=MESH)
        pl.semaphore_signal(barrier, inc=1, device_id={"tgt": across}, device_id_type=MESH)
        for i in range(1, n_blk):
            pl.semaphore_signal(
                barrier, inc=1, device_id={"blk": (b + i) % n_blk}, device_id_type=MESH
            )
        pl.semaphore_wait(barrier, n_blk + 1)

        def span(i):
            return ((b // dests + 1 + i) % steps) * rows

        def first(i, far):
            side = 1 - y if far else y
            return pltpu.make_async_remote_copy(
                src_ref=part.at[pl.ds((side * 2 + 1 - c) * own_rows + span(i), rows)],
                dst_ref=r1.at[far, pl.ds(span(i), rows)],
                send_sem=s1_send.at[far, i],
                recv_sem=s1_recv.at[far, i],
                device_id={"tgt": sibling},
                device_id_type=MESH,
            )

        def second(i):
            return pltpu.make_async_remote_copy(
                src_ref=s2.at[pl.ds(span(i), rows)],
                dst_ref=r2.at[pl.ds(span(i), rows)],
                send_sem=s2_send.at[i],
                recv_sem=s2_recv.at[i],
                device_id={"tgt": across},
                device_id_type=MESH,
            )

        def third(dest):
            return pltpu.make_async_remote_copy(
                src_ref=mine.at[pl.ds(dest * per, per)],
                dst_ref=out.at[pl.ds(b * per, per)],
                send_sem=s3_send.at[dest],
                recv_sem=s3_recv.at[b],
                device_id={"blk": dest},
                device_id_type=MESH,
            )

        def third_in(src):
            return pltpu.make_async_remote_copy(
                src_ref=mine.at[pl.ds(src * per, per)],
                dst_ref=out.at[pl.ds(src * per, per)],
                send_sem=s3_send.at[src],
                recv_sem=s3_recv.at[src],
                device_id={"blk": src},
                device_id_type=MESH,
            )

        def places(dest, slot):
            return pltpu.make_async_remote_copy(
                src_ref=pos_ref.at[dest],
                dst_ref=pos_out.at[slot],
                send_sem=p_send.at[dest],
                recv_sem=p_recv.at[slot],
                device_id={"blk": dest},
                device_id_type=MESH,
            )

        own_out = pltpu.make_async_copy(
            mine.at[pl.ds(b * per, per)], out.at[pl.ds(b * per, per)], own_sem.at[0]
        )
        own_pos = pltpu.make_async_copy(pos_ref.at[b], pos_out.at[b], own_sem.at[1])

        for i in range(steps):
            first(i, 1).start()
            first(i, 0).start()
        own_pos.start()
        for i in range(1, n_blk):
            places((b + i) % n_blk, b).start()

        def dest_of(i, j):
            return ((b // dests + 1 + i) % steps) * dests + (b % dests + j) % dests

        def finish(i):
            second(i).wait_recv()
            at = pl.ds(span(i), rows)
            mine[at] = mine[at] + r2[at]
            for j in range(dests):
                if i == steps - 1 and j == 0:
                    own_out.start()
                else:
                    third(dest_of(i, j)).start()

        for i in range(steps):
            at = pl.ds(span(i), rows)
            first(i, 1).wait_recv()
            s2[at] = part[pl.ds(((1 - y) * 2 + c) * own_rows + span(i), rows)] + r1[1, at]
            second(i).start()
            first(i, 0).wait_recv()
            mine[at] = part[pl.ds((y * 2 + c) * own_rows + span(i), rows)] + r1[0, at]
            if i >= LAG:
                finish(i - LAG)
        for i in range(max(0, steps - LAG), steps):
            finish(i)

        for i in range(steps):
            first(i, 1).wait_send()
            first(i, 0).wait_send()
            second(i).wait_send()
        for i in range(1, n_blk):
            peer = (b + i) % n_blk
            places(peer, b).wait_send()
            places(peer, peer).wait_recv()
            third(peer).wait_send()
            third_in(peer).wait_recv()
        own_pos.wait()
        own_out.wait()

    vmem = pl.BlockSpec(memory_space=pltpu.VMEM)
    dma = pltpu.SemaphoreType.DMA
    block = (own_rows, size, size)
    return pl.pallas_call(
        kernel,
        out_shape=(
            jax.ShapeDtypeStruct(block, jnp.float32),
            jax.ShapeDtypeStruct(pos.shape, jnp.int32),
        ),
        in_specs=[vmem, vmem],
        out_specs=(vmem, vmem),
        scratch_shapes=[
            pltpu.VMEM((2,) + block, jnp.float32),
            pltpu.VMEM(block, jnp.float32),
            pltpu.VMEM(block, jnp.float32),
            pltpu.VMEM(block, jnp.float32),
            dma((2, steps)), dma((2, steps)),
            dma((steps,)), dma((steps,)),
            dma((n_blk,)), dma((n_blk,)),
            dma((n_blk,)), dma((n_blk,)),
            dma((2,)),
        ],
        compiler_params=pltpu.CompilerParams(
            collective_id=0, has_side_effects=True, vmem_limit_bytes=40 << 20
        ),
    )(partial, pos)


def arrange(blocks, target):
    n = blocks.shape[0]

    def kernel(target_ref, src, dst, sem):
        @pl.loop(0, n)
        def _(r):
            pltpu.make_async_copy(src.at[r], dst.at[target_ref[r]], sem).start()

        pltpu.make_async_copy(src, dst, sem).wait()

    hbm = pl.BlockSpec(memory_space=pl.ANY)
    return pl.pallas_call(
        kernel,
        out_shape=jax.ShapeDtypeStruct(blocks.shape, blocks.dtype),
        in_specs=[pl.BlockSpec(memory_space=pltpu.SMEM), hbm],
        out_specs=hbm,
        scratch_shapes=[pltpu.SemaphoreType.DMA],
    )(target, blocks)


def on_device(integrals, densities, entry_block, entry_state, entry_slot, counts, owner):
    hb_rows = owner.shape[0]
    n_tgt = lax.axis_size("tgt")
    n_blk = lax.axis_size("blk")
    own_rows = hb_rows // n_tgt
    per = own_rows // n_blk
    piece = lax.all_gather(densities, "tgt", axis=0, tiled=True)
    keys, n_steps, st_bits, blk_bits = make_keys(
        entry_block, entry_state, entry_slot, jnp.sum(counts[0]), hb_rows,
        integrals.shape[0], piece.shape[0],
    )
    place = jnp.sum((owner[None, :] < owner[:, None]).astype(jnp.int32), axis=1)
    partial = accumulate(n_steps, keys, place, integrals, piece, st_bits, blk_bits, hb_rows)
    ranks = lax.axis_index("tgt") * own_rows + jnp.arange(own_rows, dtype=jnp.int32)
    hit = (place[None, :] == ranks[:, None]).astype(jnp.int32)
    local = jnp.sum(hit * (owner % own_rows)[None, :], axis=1).reshape(n_blk, 1, per)
    pos = jnp.pad(local, ((0, 0), (0, 7), (0, 128 - per)))
    got, got_pos = exchange(partial, pos, own_rows, n_blk)
    return arrange(got, got_pos[:, 0, :per].reshape(own_rows))


def solution(mesh):
    in_specs = (
        P(("tgt", "blk"), None, None),
        P("tgt", None, None),
        P(("tgt", "blk")),
        P(("tgt", "blk")),
        P(("tgt", "blk")),
        P(("tgt", "blk"), None),
        P("blk"),
    )
    out_specs = P(("tgt", "blk"), None, None)
    return jax.shard_map(
        on_device, mesh=mesh, in_specs=in_specs, out_specs=out_specs, check_vma=False
    )
```

```python
import jax
import jax.numpy as jnp
from jax import lax
from jax.experimental import pallas as pl
from jax.experimental.pallas import tpu as pltpu
from jax.sharding import PartitionSpec as P

CHUNK = 4
UNROLL = 2
STEPS = 8
LAG = 1
MESH = pl.DeviceIdType.MESH


def bits_for(n):
    return max(1, (n - 1).bit_length())


def accumulate(n_steps, keys, place, integrals, densities, st_bits, blk_bits, hb_rows):
    states, size, _ = densities.shape
    held = integrals.shape[0]
    st_mask = (1 << st_bits) - 1
    blk_mask = (1 << blk_bits) - 1

    def kernel(n_ref, keys_ref, place_ref, int_hbm, den_hbm, acc, ints, dens, sems):
        load_ints = pltpu.make_async_copy(int_hbm, ints, sems.at[0])
        load_dens = pltpu.make_async_copy(den_hbm, dens.at[pl.ds(0, states)], sems.at[1])
        load_ints.start()
        load_dens.start()
        dens[states] = jnp.zeros((size, size), dens.dtype)

        @pl.loop(0, hb_rows)
        def _(j):
            acc[j] = jnp.zeros((size, size), jnp.float32)

        load_ints.wait()
        load_dens.wait()

        @pl.loop(0, n_ref[0])
        def _(step):
            prods = []
            for u in range(UNROLL):
                base = (step * UNROLL + u) * CHUNK
                ks = [keys_ref[base + i] for i in range(CHUNK)]
                lhs = jnp.concatenate([ints[(k >> st_bits) & blk_mask] for k in ks], axis=1)
                rhs = jnp.concatenate([dens[k & st_mask] for k in ks], axis=0)
                row = place_ref[ks[0] >> (st_bits + blk_bits)]
                prods.append((row, jnp.dot(lhs, rhs, preferred_element_type=jnp.float32)))
            for row, prod in prods:
                acc[row] += prod

    smem = pl.BlockSpec(memory_space=pltpu.SMEM)
    hbm = pl.BlockSpec(memory_space=pl.ANY)
    return pl.pallas_call(
        kernel,
        out_shape=jax.ShapeDtypeStruct((hb_rows, size, size), jnp.float32),
        in_specs=[smem, smem, smem, hbm, hbm],
        out_specs=pl.BlockSpec(memory_space=pltpu.VMEM),
        scratch_shapes=[
            pltpu.VMEM((held, size, size), integrals.dtype),
            pltpu.VMEM((states + 1, size, size), densities.dtype),
            pltpu.SemaphoreType.DMA((2,)),
        ],
        compiler_params=pltpu.CompilerParams(vmem_limit_bytes=40 << 20),
    )(n_steps, keys, place, integrals, densities)


def make_keys(entry_block, entry_state, entry_slot, live, hb_rows, held, states):
    st_bits = bits_for(states + 1)
    blk_bits = bits_for(held)
    e_cap = entry_block.shape[0]
    valid = jnp.arange(e_cap, dtype=jnp.int32) < live
    slots = jnp.arange(hb_rows, dtype=jnp.int32)
    per_slot = jnp.sum(
        ((entry_slot[:, None] == slots[None, :]) & valid[:, None]).astype(jnp.int32), axis=0
    )
    spare = (-per_slot) % CHUNK
    filler = (slots << (st_bits + blk_bits)) + ((held - 1) << st_bits) + states
    last = filler[hb_rows - 1]
    key = (((entry_slot << blk_bits) + entry_block) << st_bits) + entry_state
    key = jnp.where(valid, key, last)
    order = jnp.arange(CHUNK - 1, dtype=jnp.int32)
    fill = jnp.where(order[:, None] < spare[None, :], filler[None, :], last).reshape(-1)
    total = e_cap + fill.shape[0]
    group = CHUNK * UNROLL
    tail = jnp.full(((-total) % group,), last, jnp.int32)
    keys = lax.sort(jnp.concatenate([key, fill, tail]))
    n_steps = (jnp.sum(per_slot + spare) + group - 1) // group
    return keys, n_steps.reshape(1), st_bits, blk_bits


def exchange(partial, pos, own_rows, n_blk):
    size = partial.shape[-1]
    steps = min(STEPS, n_blk)
    rows = own_rows // steps
    dests = n_blk // steps
    per = own_rows // n_blk

    def kernel(part, pos_ref, out, pos_out, r1, s2, r2, mine,
               s1_send, s1_recv, s2_send, s2_recv, s3_send, s3_recv, p_send, p_recv, own_sem):
        t = lax.axis_index("tgt")
        b = lax.axis_index("blk")
        y, c = t // 2, t % 2
        sibling = y * 2 + (1 - c)
        across = (1 - y) * 2 + c
        barrier = pltpu.get_barrier_semaphore()
        pl.semaphore_signal(barrier, inc=1, device_id={"tgt": sibling}, device_id_type=MESH)
        pl.semaphore_signal(barrier, inc=1, device_id={"tgt": across}, device_id_type=MESH)
        for i in range(1, n_blk):
            pl.semaphore_signal(
                barrier, inc=1, device_id={"blk": (b + i) % n_blk}, device_id_type=MESH
            )
        pl.semaphore_wait(barrier, n_blk + 1)

        def span(i):
            return ((b // dests + 1 + i) % steps) * rows

        def first(i, far):
            side = 1 - y if far else y
            return pltpu.make_async_remote_copy(
                src_ref=part.at[pl.ds((side * 2 + 1 - c) * own_rows + span(i), rows)],
                dst_ref=r1.at[far, pl.ds(span(i), rows)],
                send_sem=s1_send.at[far, i],
                recv_sem=s1_recv.at[far, i],
                device_id={"tgt": sibling},
                device_id_type=MESH,
            )

        def second(i):
            return pltpu.make_async_remote_copy(
                src_ref=s2.at[pl.ds(span(i), rows)],
                dst_ref=r2.at[pl.ds(span(i), rows)],
                send_sem=s2_send.at[i],
                recv_sem=s2_recv.at[i],
                device_id={"tgt": across},
                device_id_type=MESH,
            )

        def third(dest):
            return pltpu.make_async_remote_copy(
                src_ref=mine.at[pl.ds(dest * per, per)],
                dst_ref=out.at[pl.ds(b * per, per)],
                send_sem=s3_send.at[dest],
                recv_sem=s3_recv.at[b],
                device_id={"blk": dest},
                device_id_type=MESH,
            )

        def third_in(src):
            return pltpu.make_async_remote_copy(
                src_ref=mine.at[pl.ds(src * per, per)],
                dst_ref=out.at[pl.ds(src * per, per)],
                send_sem=s3_send.at[src],
                recv_sem=s3_recv.at[src],
                device_id={"blk": src},
                device_id_type=MESH,
            )

        def places(dest, slot):
            return pltpu.make_async_remote_copy(
                src_ref=pos_ref.at[dest],
                dst_ref=pos_out.at[slot],
                send_sem=p_send.at[dest],
                recv_sem=p_recv.at[slot],
                device_id={"blk": dest},
                device_id_type=MESH,
            )

        own_out = pltpu.make_async_copy(
            mine.at[pl.ds(b * per, per)], out.at[pl.ds(b * per, per)], own_sem.at[0]
        )
        own_pos = pltpu.make_async_copy(pos_ref.at[b], pos_out.at[b], own_sem.at[1])

        for i in range(steps):
            first(i, 1).start()
            first(i, 0).start()
        own_pos.start()
        for i in range(1, n_blk):
            places((b + i) % n_blk, b).start()

        def dest_of(i, j):
            return ((b // dests + 1 + i) % steps) * dests + (b % dests + j) % dests

        def finish(i):
            second(i).wait_recv()
            at = pl.ds(span(i), rows)
            mine[at] = mine[at] + r2[at]
            for j in range(dests):
                if i == steps - 1 and j == 0:
                    own_out.start()
                else:
                    third(dest_of(i, j)).start()

        for i in range(steps):
            at = pl.ds(span(i), rows)
            first(i, 1).wait_recv()
            s2[at] = part[pl.ds(((1 - y) * 2 + c) * own_rows + span(i), rows)] + r1[1, at]
            second(i).start()
            first(i, 0).wait_recv()
            mine[at] = part[pl.ds((y * 2 + c) * own_rows + span(i), rows)] + r1[0, at]
            if i >= LAG:
                finish(i - LAG)
        for i in range(max(0, steps - LAG), steps):
            finish(i)

        for i in range(steps):
            first(i, 1).wait_send()
            first(i, 0).wait_send()
            second(i).wait_send()
        for i in range(1, n_blk):
            peer = (b + i) % n_blk
            places(peer, b).wait_send()
            places(peer, peer).wait_recv()
            third(peer).wait_send()
            third_in(peer).wait_recv()
        own_pos.wait()
        own_out.wait()

    vmem = pl.BlockSpec(memory_space=pltpu.VMEM)
    dma = pltpu.SemaphoreType.DMA
    block = (own_rows, size, size)
    return pl.pallas_call(
        kernel,
        out_shape=(
            jax.ShapeDtypeStruct(block, jnp.float32),
            jax.ShapeDtypeStruct(pos.shape, jnp.int32),
        ),
        in_specs=[vmem, vmem],
        out_specs=(vmem, vmem),
        scratch_shapes=[
            pltpu.VMEM((2,) + block, jnp.float32),
            pltpu.VMEM(block, jnp.float32),
            pltpu.VMEM(block, jnp.float32),
            pltpu.VMEM(block, jnp.float32),
            dma((2, steps)), dma((2, steps)),
            dma((steps,)), dma((steps,)),
            dma((n_blk,)), dma((n_blk,)),
            dma((n_blk,)), dma((n_blk,)),
            dma((2,)),
        ],
        compiler_params=pltpu.CompilerParams(
            collective_id=0, has_side_effects=True, vmem_limit_bytes=40 << 20
        ),
    )(partial, pos)


def arrange(blocks, target):
    n = blocks.shape[0]

    def kernel(target_ref, src, dst, sem):
        @pl.loop(0, n)
        def _(r):
            pltpu.make_async_copy(src.at[r], dst.at[target_ref[r]], sem).start()

        pltpu.make_async_copy(src, dst, sem).wait()

    hbm = pl.BlockSpec(memory_space=pl.ANY)
    return pl.pallas_call(
        kernel,
        out_shape=jax.ShapeDtypeStruct(blocks.shape, blocks.dtype),
        in_specs=[pl.BlockSpec(memory_space=pltpu.SMEM), pl.BlockSpec(memory_space=pltpu.VMEM)],
        out_specs=hbm,
        scratch_shapes=[pltpu.SemaphoreType.DMA],
    )(target, blocks)


def on_device(integrals, densities, entry_block, entry_state, entry_slot, counts, owner):
    hb_rows = owner.shape[0]
    n_tgt = lax.axis_size("tgt")
    n_blk = lax.axis_size("blk")
    own_rows = hb_rows // n_tgt
    per = own_rows // n_blk
    piece = lax.all_gather(densities, "tgt", axis=0, tiled=True)
    keys, n_steps, st_bits, blk_bits = make_keys(
        entry_block, entry_state, entry_slot, jnp.sum(counts[0]), hb_rows,
        integrals.shape[0], piece.shape[0],
    )
    place = jnp.sum((owner[None, :] < owner[:, None]).astype(jnp.int32), axis=1)
    partial = accumulate(n_steps, keys, place, integrals, piece, st_bits, blk_bits, hb_rows)
    ranks = lax.axis_index("tgt") * own_rows + jnp.arange(own_rows, dtype=jnp.int32)
    hit = (place[None, :] == ranks[:, None]).astype(jnp.int32)
    local = jnp.sum(hit * (owner % own_rows)[None, :], axis=1).reshape(n_blk, 1, per)
    pos = jnp.pad(local, ((0, 0), (0, 7), (0, 128 - per)))
    got, got_pos = exchange(partial, pos, own_rows, n_blk)
    return arrange(got, got_pos[:, 0, :per].reshape(own_rows))


def solution(mesh):
    in_specs = (
        P(("tgt", "blk"), None, None),
        P("tgt", None, None),
        P(("tgt", "blk")),
        P(("tgt", "blk")),
        P(("tgt", "blk")),
        P(("tgt", "blk"), None),
        P("blk"),
    )
    out_specs = P(("tgt", "blk"), None, None)
    return jax.shard_map(
        on_device, mesh=mesh, in_specs=in_specs, out_specs=out_specs, check_vma=False
    )
```

```python
import jax
import jax.numpy as jnp
from jax import lax
from jax.experimental import pallas as pl
from jax.experimental.pallas import tpu as pltpu
from jax.sharding import PartitionSpec as P

CHUNK = 4
UNROLL = 4
STEPS = 8
LAG = 1
MESH = pl.DeviceIdType.MESH


def bits_for(n):
    return max(1, (n - 1).bit_length())


def accumulate(n_steps, keys, place, integrals, densities, st_bits, blk_bits, hb_rows):
    states, size, _ = densities.shape
    held = integrals.shape[0]
    st_mask = (1 << st_bits) - 1
    blk_mask = (1 << blk_bits) - 1

    def kernel(n_ref, keys_ref, place_ref, int_hbm, den_hbm, acc, ints, dens, sems):
        load_ints = pltpu.make_async_copy(int_hbm, ints, sems.at[0])
        load_dens = pltpu.make_async_copy(den_hbm, dens.at[pl.ds(0, states)], sems.at[1])
        load_ints.start()
        load_dens.start()
        dens[states] = jnp.zeros((size, size), dens.dtype)

        @pl.loop(0, hb_rows)
        def _(j):
            acc[j] = jnp.zeros((size, size), jnp.float32)

        load_ints.wait()
        load_dens.wait()

        @pl.loop(0, n_ref[0])
        def _(step):
            prods = []
            for u in range(UNROLL):
                base = (step * UNROLL + u) * CHUNK
                ks = [keys_ref[base + i] for i in range(CHUNK)]
                lhs = jnp.concatenate([ints[(k >> st_bits) & blk_mask] for k in ks], axis=1)
                rhs = jnp.concatenate([dens[k & st_mask] for k in ks], axis=0)
                row = place_ref[ks[0] >> (st_bits + blk_bits)]
                prods.append((row, jnp.dot(lhs, rhs, preferred_element_type=jnp.float32)))
            for row, prod in prods:
                acc[row] += prod

    smem = pl.BlockSpec(memory_space=pltpu.SMEM)
    hbm = pl.BlockSpec(memory_space=pl.ANY)
    return pl.pallas_call(
        kernel,
        out_shape=jax.ShapeDtypeStruct((hb_rows, size, size), jnp.float32),
        in_specs=[smem, smem, smem, hbm, hbm],
        out_specs=pl.BlockSpec(memory_space=pltpu.VMEM),
        scratch_shapes=[
            pltpu.VMEM((held, size, size), integrals.dtype),
            pltpu.VMEM((states + 1, size, size), densities.dtype),
            pltpu.SemaphoreType.DMA((2,)),
        ],
        compiler_params=pltpu.CompilerParams(vmem_limit_bytes=40 << 20),
    )(n_steps, keys, place, integrals, densities)


def make_keys(entry_block, entry_state, entry_slot, live, hb_rows, held, states):
    st_bits = bits_for(states + 1)
    blk_bits = bits_for(held)
    e_cap = entry_block.shape[0]
    valid = jnp.arange(e_cap, dtype=jnp.int32) < live
    slots = jnp.arange(hb_rows, dtype=jnp.int32)
    per_slot = jnp.sum(
        ((entry_slot[:, None] == slots[None, :]) & valid[:, None]).astype(jnp.int32), axis=0
    )
    spare = (-per_slot) % CHUNK
    filler = (slots << (st_bits + blk_bits)) + ((held - 1) << st_bits) + states
    last = filler[hb_rows - 1]
    key = (((entry_slot << blk_bits) + entry_block) << st_bits) + entry_state
    key = jnp.where(valid, key, last)
    order = jnp.arange(CHUNK - 1, dtype=jnp.int32)
    fill = jnp.where(order[:, None] < spare[None, :], filler[None, :], last).reshape(-1)
    total = e_cap + fill.shape[0]
    group = CHUNK * UNROLL
    tail = jnp.full(((-total) % group,), last, jnp.int32)
    keys = lax.sort(jnp.concatenate([key, fill, tail]))
    n_steps = (jnp.sum(per_slot + spare) + group - 1) // group
    return keys, n_steps.reshape(1), st_bits, blk_bits


LEVELS = 32767.0
SMALLEST = 1e-33


def narrow(x):
    top = jnp.maximum(jnp.max(jnp.abs(x), axis=0, keepdims=True), SMALLEST)
    return jnp.round(x * (LEVELS / top)).astype(jnp.int32).astype(jnp.int16), top * (1.0 / LEVELS)


def widen(q, step):
    return q.astype(jnp.int32).astype(jnp.float32) * step


def exchange(partial, pos, own_rows, n_blk):
    size = partial.shape[-1]
    steps = min(STEPS, n_blk)
    rows = own_rows // steps
    dests = n_blk // steps
    per = own_rows // n_blk

    def kernel(part, pos_ref, out, step_out, r1, s2, r2, s3, step2, step2_in, step3,
               s1_send, s1_recv, s2_send, s2_recv, t2_send, t2_recv, s3_send, s3_recv,
               t3_send, t3_recv, own_sem):
        t = lax.axis_index("tgt")
        b = lax.axis_index("blk")
        y, c = t // 2, t % 2
        sibling = y * 2 + (1 - c)
        across = (1 - y) * 2 + c
        barrier = pltpu.get_barrier_semaphore()
        pl.semaphore_signal(barrier, inc=1, device_id={"tgt": sibling}, device_id_type=MESH)
        pl.semaphore_signal(barrier, inc=1, device_id={"tgt": across}, device_id_type=MESH)
        for i in range(1, n_blk):
            pl.semaphore_signal(
                barrier, inc=1, device_id={"blk": (b + i) % n_blk}, device_id_type=MESH
            )
        pl.semaphore_wait(barrier, n_blk + 1)

        def span(i):
            return ((b // dests + 1 + i) % steps) * rows

        def first(i, far):
            side = 1 - y if far else y
            return pltpu.make_async_remote_copy(
                src_ref=part.at[pl.ds((side * 2 + 1 - c) * own_rows + span(i), rows)],
                dst_ref=r1.at[far, pl.ds(span(i), rows)],
                send_sem=s1_send.at[far, i],
                recv_sem=s1_recv.at[far, i],
                device_id={"tgt": sibling},
                device_id_type=MESH,
            )

        def second(i):
            return pltpu.make_async_remote_copy(
                src_ref=s2.at[pl.ds(span(i), rows)],
                dst_ref=r2.at[pl.ds(span(i), rows)],
                send_sem=s2_send.at[i],
                recv_sem=s2_recv.at[i],
                device_id={"tgt": across},
                device_id_type=MESH,
            )

        def second_steps(i):
            return pltpu.make_async_remote_copy(
                src_ref=step2.at[i],
                dst_ref=step2_in.at[i],
                send_sem=t2_send.at[i],
                recv_sem=t2_recv.at[i],
                device_id={"tgt": across},
                device_id_type=MESH,
            )

        def third(dest, slot):
            return pltpu.make_async_remote_copy(
                src_ref=s3.at[pl.ds(dest * per, per)],
                dst_ref=out.at[pl.ds(slot * per, per)],
                send_sem=s3_send.at[dest],
                recv_sem=s3_recv.at[slot],
                device_id={"blk": dest},
                device_id_type=MESH,
            )

        def third_steps(dest, slot):
            return pltpu.make_async_remote_copy(
                src_ref=step3.at[dest],
                dst_ref=step_out.at[slot],
                send_sem=t3_send.at[dest],
                recv_sem=t3_recv.at[slot],
                device_id={"blk": dest},
                device_id_type=MESH,
            )

        own_out = pltpu.make_async_copy(
            s3.at[pl.ds(b * per, per)], out.at[pl.ds(b * per, per)], own_sem.at[0]
        )
        own_steps = pltpu.make_async_copy(step3.at[b], step_out.at[b], own_sem.at[1])

        for i in range(steps):
            first(i, 1).start()
            first(i, 0).start()

        def finish(i):
            first(i, 0).wait_recv()
            second(i).wait_recv()
            second_steps(i).wait_recv()
            steps_in = step2_in[i]
            for j in range(dests):
                dest = ((b // dests + 1 + i) % steps) * dests + (b % dests + j) % dests
                step3[dest] = pos_ref[dest]
                for k in range(per):
                    row = dest * per + k
                    at = ((b % dests + j) % dests) * per + k if dests > 1 else k
                    if dests > 1:
                        scale = step2_in[i, pl.ds(at, 1), :]
                    else:
                        scale = steps_in[k:k + 1]
                    total = part[(y * 2 + c) * own_rows + row] + r1[0, row] + widen(r2[row], scale)
                    q, step = narrow(total)
                    s3[row] = q
                    step3[dest, k:k + 1, :] = step
                if i == steps - 1 and j == 0:
                    own_out.start()
                    own_steps.start()
                else:
                    third(dest, b).start()
                    third_steps(dest, b).start()

        for i in range(steps):
            first(i, 1).wait_recv()
            for k in range(rows):
                row = span(i) + k
                q, step = narrow(part[((1 - y) * 2 + c) * own_rows + row] + r1[1, row])
                s2[row] = q
                step2[i, k:k + 1, :] = step
            for k in range(rows, 8):
                step2[i, k:k + 1, :] = jnp.zeros((1, size), jnp.float32)
            second(i).start()
            second_steps(i).start()
            if i >= LAG:
                finish(i - LAG)
        for i in range(max(0, steps - LAG), steps):
            finish(i)

        for i in range(steps):
            first(i, 1).wait_send()
            first(i, 0).wait_send()
            second(i).wait_send()
            second_steps(i).wait_send()
        for i in range(1, n_blk):
            peer = (b + i) % n_blk
            third(peer, b).wait_send()
            third_steps(peer, b).wait_send()
            third(peer, peer).wait_recv()
            third_steps(peer, peer).wait_recv()
        own_steps.wait()
        own_out.wait()

    vmem = pl.BlockSpec(memory_space=pltpu.VMEM)
    dma = pltpu.SemaphoreType.DMA
    block = (own_rows, size, size)
    return pl.pallas_call(
        kernel,
        out_shape=(
            jax.ShapeDtypeStruct(block, jnp.int16),
            jax.ShapeDtypeStruct(pos.shape, jnp.float32),
        ),
        in_specs=[vmem, vmem],
        out_specs=(vmem, vmem),
        scratch_shapes=[
            pltpu.VMEM((2,) + block, jnp.float32),
            pltpu.VMEM(block, jnp.int16),
            pltpu.VMEM(block, jnp.int16),
            pltpu.VMEM(block, jnp.int16),
            pltpu.VMEM((steps, 8, size), jnp.float32),
            pltpu.VMEM((steps, 8, size), jnp.float32),
            pltpu.VMEM((n_blk, 8, size), jnp.float32),
            dma((2, steps)), dma((2, steps)),
            dma((steps,)), dma((steps,)),
            dma((steps,)), dma((steps,)),
            dma((n_blk,)), dma((n_blk,)),
            dma((n_blk,)), dma((n_blk,)),
            dma((2,)),
        ],
        compiler_params=pltpu.CompilerParams(
            collective_id=0, has_side_effects=True, vmem_limit_bytes=40 << 20
        ),
    )(partial, pos)


def arrange(blocks, sizes, target):
    n, size, _ = blocks.shape
    n_blk = sizes.shape[0]
    per = n // n_blk

    def kernel(target_ref, src, sizes_ref, dst, wide, sem):
        @pl.loop(0, n_blk)
        def _(s):
            for k in range(per):
                r = s * per + k
                wide[r] = widen(src[r], sizes_ref[s, k:k + 1, :])
                pltpu.make_async_copy(wide.at[r], dst.at[target_ref[r]], sem).start()

        pltpu.make_async_copy(wide, dst, sem).wait()

    vmem = pl.BlockSpec(memory_space=pltpu.VMEM)
    return pl.pallas_call(
        kernel,
        out_shape=jax.ShapeDtypeStruct(blocks.shape, jnp.float32),
        in_specs=[pl.BlockSpec(memory_space=pltpu.SMEM), vmem, vmem],
        out_specs=pl.BlockSpec(memory_space=pl.ANY),
        scratch_shapes=[pltpu.VMEM(blocks.shape, jnp.float32), pltpu.SemaphoreType.DMA],
    )(target, blocks, sizes)


def on_device(integrals, densities, entry_block, entry_state, entry_slot, counts, owner):
    hb_rows = owner.shape[0]
    n_tgt = lax.axis_size("tgt")
    n_blk = lax.axis_size("blk")
    own_rows = hb_rows // n_tgt
    per = own_rows // n_blk
    piece = lax.all_gather(densities, "tgt", axis=0, tiled=True)
    keys, n_steps, st_bits, blk_bits = make_keys(
        entry_block, entry_state, entry_slot, jnp.sum(counts[0]), hb_rows,
        integrals.shape[0], piece.shape[0],
    )
    place = jnp.sum((owner[None, :] < owner[:, None]).astype(jnp.int32), axis=1)
    partial = accumulate(n_steps, keys, place, integrals, piece, st_bits, blk_bits, hb_rows)
    ranks = lax.axis_index("tgt") * own_rows + jnp.arange(own_rows, dtype=jnp.int32)
    hit = (place[None, :] == ranks[:, None]).astype(jnp.int32)
    local = jnp.sum(hit * (owner % own_rows)[None, :], axis=1).reshape(n_blk, 1, per)
    pos = jnp.pad(local, ((0, 0), (7, 0), (0, integrals.shape[1] - per))).astype(jnp.float32)
    got, sizes = exchange(partial, pos, own_rows, n_blk)
    return arrange(got, sizes, sizes[:, 7, :per].astype(jnp.int32).reshape(own_rows))


def solution(mesh):
    in_specs = (
        P(("tgt", "blk"), None, None),
        P("tgt", None, None),
        P(("tgt", "blk")),
        P(("tgt", "blk")),
        P(("tgt", "blk")),
        P(("tgt", "blk"), None),
        P("blk"),
    )
    out_specs = P(("tgt", "blk"), None, None)
    return jax.shard_map(
        on_device, mesh=mesh, in_specs=in_specs, out_specs=out_specs, check_vma=False
    )
```

```python
import jax
import jax.numpy as jnp
from jax import lax
from jax.experimental import pallas as pl
from jax.experimental.pallas import tpu as pltpu
from jax.sharding import PartitionSpec as P

CHUNK = 4
UNROLL = 8
STEPS = 8
LAG = 1
MESH = pl.DeviceIdType.MESH


def bits_for(n):
    return max(1, (n - 1).bit_length())


def accumulate(n_steps, keys, place, integrals, pieces, groups, st_bits, blk_bits, hb_rows):
    s_group, size, _ = pieces[0].shape
    states = s_group * len(pieces)
    st_mask = (1 << st_bits) - 1
    blk_mask = (1 << blk_bits) - 1

    def kernel(n_ref, keys_ref, place_ref, groups_ref, ints, *rest):
        den_refs, (acc, dens, sems) = rest[:len(pieces)], rest[len(pieces):]
        loads = [
            pltpu.make_async_copy(
                ref, dens.at[pl.ds(groups_ref[i] * s_group, s_group)], sems.at[i]
            )
            for i, ref in enumerate(den_refs)
        ]
        for load in loads:
            load.start()
        dens[states] = jnp.zeros((size, size), dens.dtype)

        @pl.loop(0, hb_rows)
        def _(j):
            acc[j] = jnp.zeros((size, size), jnp.float32)

        for load in loads:
            load.wait()

        @pl.loop(0, n_ref[0])
        def _(step):
            prods = []
            for u in range(UNROLL):
                base = (step * UNROLL + u) * CHUNK
                ks = [keys_ref[base + i] for i in range(CHUNK)]
                lhs = jnp.concatenate([ints[(k >> st_bits) & blk_mask] for k in ks], axis=1)
                rhs = jnp.concatenate([dens[k & st_mask] for k in ks], axis=0)
                row = place_ref[ks[0] >> (st_bits + blk_bits)]
                prods.append((row, jnp.dot(lhs, rhs, preferred_element_type=jnp.float32)))
            for row, prod in prods:
                acc[row] += prod

    smem = pl.BlockSpec(memory_space=pltpu.SMEM)
    vmem = pl.BlockSpec(memory_space=pltpu.VMEM)
    hbm = pl.BlockSpec(memory_space=pl.ANY)
    return pl.pallas_call(
        kernel,
        out_shape=jax.ShapeDtypeStruct((hb_rows, size, size), jnp.float32),
        in_specs=[smem] * 4 + [vmem] + [hbm] * len(pieces),
        out_specs=vmem,
        scratch_shapes=[
            pltpu.VMEM((states + 1, size, size), pieces[0].dtype),
            pltpu.SemaphoreType.DMA((len(pieces),)),
        ],
        compiler_params=pltpu.CompilerParams(vmem_limit_bytes=32 << 20),
    )(n_steps, keys, place, groups, integrals, *pieces)


def make_keys(entry_block, entry_state, entry_slot, live, hb_rows, held, states):
    st_bits = bits_for(states + 1)
    blk_bits = bits_for(held)
    e_cap = entry_block.shape[0]
    valid = jnp.arange(e_cap, dtype=jnp.int32) < live
    slots = jnp.arange(hb_rows, dtype=jnp.int32)
    per_slot = jnp.sum(
        ((entry_slot[:, None] == slots[None, :]) & valid[:, None]).astype(jnp.int32), axis=0
    )
    spare = (-per_slot) % CHUNK
    filler = (slots << (st_bits + blk_bits)) + ((held - 1) << st_bits) + states
    last = filler[hb_rows - 1]
    key = (((entry_slot << blk_bits) + entry_block) << st_bits) + entry_state
    key = jnp.where(valid, key, last)
    order = jnp.arange(CHUNK - 1, dtype=jnp.int32)
    fill = jnp.where(order[:, None] < spare[None, :], filler[None, :], last).reshape(-1)
    total = e_cap + fill.shape[0]
    group = CHUNK * UNROLL
    tail = jnp.full(((-total) % group,), last, jnp.int32)
    keys = lax.sort(jnp.concatenate([key, fill, tail]), is_stable=False)
    n_steps = (jnp.sum(per_slot + spare) + group - 1) // group
    return keys, n_steps.reshape(1), st_bits, blk_bits


LEVELS = 32767.0
SMALLEST = 1e-33


def narrow(x):
    top = jnp.maximum(jnp.max(jnp.abs(x), axis=0, keepdims=True), SMALLEST)
    return jnp.round(x * (LEVELS / top)).astype(jnp.int32).astype(jnp.int16), top * (1.0 / LEVELS)


def widen(q, step):
    return q.astype(jnp.int32).astype(jnp.float32) * step


def exchange(partial, pos, own_rows, n_blk):
    size = partial.shape[-1]
    steps = min(STEPS, n_blk)
    rows = own_rows // steps
    dests = n_blk // steps
    per = own_rows // n_blk

    def kernel(part, pos_ref, out, step_out, r1, s2, r2, s3, step2, step2_in, step3,
               s1_send, s1_recv, s2_send, s2_recv, t2_send, t2_recv, s3_send, s3_recv,
               t3_send, t3_recv, own_sem):
        t = lax.axis_index("tgt")
        b = lax.axis_index("blk")
        y, c = t // 2, t % 2
        sibling = y * 2 + (1 - c)
        across = (1 - y) * 2 + c
        barrier = pltpu.get_barrier_semaphore()
        pl.semaphore_signal(barrier, inc=1, device_id={"tgt": sibling}, device_id_type=MESH)
        pl.semaphore_signal(barrier, inc=1, device_id={"tgt": across}, device_id_type=MESH)
        for i in range(1, n_blk):
            pl.semaphore_signal(
                barrier, inc=1, device_id={"blk": (b + i) % n_blk}, device_id_type=MESH
            )
        pl.semaphore_wait(barrier, n_blk + 1)

        def span(i):
            return ((b // dests + 1 + i) % steps) * rows

        def first(i, far):
            side = 1 - y if far else y
            return pltpu.make_async_remote_copy(
                src_ref=part.at[pl.ds((side * 2 + 1 - c) * own_rows + span(i), rows)],
                dst_ref=r1.at[far, pl.ds(span(i), rows)],
                send_sem=s1_send.at[far, i],
                recv_sem=s1_recv.at[far, i],
                device_id={"tgt": sibling},
                device_id_type=MESH,
            )

        def second(i):
            return pltpu.make_async_remote_copy(
                src_ref=s2.at[pl.ds(span(i), rows)],
                dst_ref=r2.at[pl.ds(span(i), rows)],
                send_sem=s2_send.at[i],
                recv_sem=s2_recv.at[i],
                device_id={"tgt": across},
                device_id_type=MESH,
            )

        def second_steps(i):
            return pltpu.make_async_remote_copy(
                src_ref=step2.at[i],
                dst_ref=step2_in.at[i],
                send_sem=t2_send.at[i],
                recv_sem=t2_recv.at[i],
                device_id={"tgt": across},
                device_id_type=MESH,
            )

        def third(dest, slot):
            return pltpu.make_async_remote_copy(
                src_ref=s3.at[pl.ds(dest * per, per)],
                dst_ref=out.at[pl.ds(slot * per, per)],
                send_sem=s3_send.at[dest],
                recv_sem=s3_recv.at[slot],
                device_id={"blk": dest},
                device_id_type=MESH,
            )

        def third_steps(dest, slot):
            return pltpu.make_async_remote_copy(
                src_ref=step3.at[dest],
                dst_ref=step_out.at[slot],
                send_sem=t3_send.at[dest],
                recv_sem=t3_recv.at[slot],
                device_id={"blk": dest},
                device_id_type=MESH,
            )

        own_out = pltpu.make_async_copy(
            s3.at[pl.ds(b * per, per)], out.at[pl.ds(b * per, per)], own_sem.at[0]
        )
        own_steps = pltpu.make_async_copy(step3.at[b], step_out.at[b], own_sem.at[1])

        for i in range(steps):
            first(i, 1).start()
            first(i, 0).start()

        def finish(i):
            first(i, 0).wait_recv()
            second(i).wait_recv()
            second_steps(i).wait_recv()
            steps_in = step2_in[i]
            for j in range(dests):
                dest = ((b // dests + 1 + i) % steps) * dests + (b % dests + j) % dests
                step3[dest] = pos_ref[dest]
                for k in range(per):
                    row = dest * per + k
                    at = ((b % dests + j) % dests) * per + k if dests > 1 else k
                    if dests > 1:
                        scale = step2_in[i, pl.ds(at, 1), :]
                    else:
                        scale = steps_in[k:k + 1]
                    total = part[(y * 2 + c) * own_rows + row] + r1[0, row] + widen(r2[row], scale)
                    q, step = narrow(total)
                    s3[row] = q
                    step3[dest, k:k + 1, :] = step
                if i == steps - 1 and j == 0:
                    own_out.start()
                    own_steps.start()
                else:
                    third(dest, b).start()
                    third_steps(dest, b).start()

        for i in range(steps):
            first(i, 1).wait_recv()
            for k in range(rows):
                row = span(i) + k
                q, step = narrow(part[((1 - y) * 2 + c) * own_rows + row] + r1[1, row])
                s2[row] = q
                step2[i, k:k + 1, :] = step
            for k in range(rows, 8):
                step2[i, k:k + 1, :] = jnp.zeros((1, size), jnp.float32)
            second(i).start()
            second_steps(i).start()
            if i >= LAG:
                finish(i - LAG)
        for i in range(max(0, steps - LAG), steps):
            finish(i)

        for i in range(steps):
            first(i, 1).wait_send()
            first(i, 0).wait_send()
            second(i).wait_send()
            second_steps(i).wait_send()
        for i in range(1, n_blk):
            peer = (b + i) % n_blk
            third(peer, b).wait_send()
            third_steps(peer, b).wait_send()
            third(peer, peer).wait_recv()
            third_steps(peer, peer).wait_recv()
        own_steps.wait()
        own_out.wait()

    vmem = pl.BlockSpec(memory_space=pltpu.VMEM)
    dma = pltpu.SemaphoreType.DMA
    block = (own_rows, size, size)
    return pl.pallas_call(
        kernel,
        out_shape=(
            jax.ShapeDtypeStruct(block, jnp.int16),
            jax.ShapeDtypeStruct(pos.shape, jnp.float32),
        ),
        in_specs=[vmem, vmem],
        out_specs=(vmem, vmem),
        scratch_shapes=[
            pltpu.VMEM((2,) + block, jnp.float32),
            pltpu.VMEM(block, jnp.int16),
            pltpu.VMEM(block, jnp.int16),
            pltpu.VMEM(block, jnp.int16),
            pltpu.VMEM((steps, 8, size), jnp.float32),
            pltpu.VMEM((steps, 8, size), jnp.float32),
            pltpu.VMEM((n_blk, 8, size), jnp.float32),
            dma((2, steps)), dma((2, steps)),
            dma((steps,)), dma((steps,)),
            dma((steps,)), dma((steps,)),
            dma((n_blk,)), dma((n_blk,)),
            dma((n_blk,)), dma((n_blk,)),
            dma((2,)),
        ],
        compiler_params=pltpu.CompilerParams(
            collective_id=0, has_side_effects=True, vmem_limit_bytes=40 << 20
        ),
    )(partial, pos)


def arrange(blocks, sizes, target):
    n, size, _ = blocks.shape
    n_blk = sizes.shape[0]
    per = n // n_blk

    def kernel(target_ref, src, sizes_ref, dst, wide, sem):
        @pl.loop(0, n_blk)
        def _(s):
            for k in range(per):
                r = s * per + k
                wide[r] = widen(src[r], sizes_ref[s, k:k + 1, :])
                pltpu.make_async_copy(wide.at[r], dst.at[target_ref[r]], sem).start()

        pltpu.make_async_copy(wide, dst, sem).wait()

    vmem = pl.BlockSpec(memory_space=pltpu.VMEM)
    return pl.pallas_call(
        kernel,
        out_shape=jax.ShapeDtypeStruct(blocks.shape, jnp.float32),
        in_specs=[pl.BlockSpec(memory_space=pltpu.SMEM), vmem, vmem],
        out_specs=pl.BlockSpec(memory_space=pl.ANY),
        scratch_shapes=[pltpu.VMEM(blocks.shape, jnp.float32), pltpu.SemaphoreType.DMA],
    )(target, blocks, sizes)


def on_device(integrals, densities, entry_block, entry_state, entry_slot, counts, owner):
    hb_rows = owner.shape[0]
    n_tgt = lax.axis_size("tgt")
    n_blk = lax.axis_size("blk")
    own_rows = hb_rows // n_tgt
    per = own_rows // n_blk
    t = lax.axis_index("tgt")
    over = [(i, i ^ 2) for i in range(n_tgt)]
    beside = [(i, i ^ 1) for i in range(n_tgt)]
    far = lax.ppermute(densities, "tgt", over)
    near = lax.ppermute(densities, "tgt", beside)
    far_near = lax.ppermute(far, "tgt", beside)
    pieces = (densities, near, far, far_near)
    groups = t ^ jnp.arange(4, dtype=jnp.int32)
    keys, n_steps, st_bits, blk_bits = make_keys(
        entry_block, entry_state, entry_slot, jnp.sum(counts[0]), hb_rows,
        integrals.shape[0], densities.shape[0] * n_tgt,
    )
    place = jnp.sum((owner[None, :] < owner[:, None]).astype(jnp.int32), axis=1)
    partial = accumulate(
        n_steps, keys, place, integrals, pieces, groups, st_bits, blk_bits, hb_rows
    )
    ranks = t * own_rows + jnp.arange(own_rows, dtype=jnp.int32)
    hit = (place[None, :] == ranks[:, None]).astype(jnp.int32)
    local = jnp.sum(hit * (owner % own_rows)[None, :], axis=1).reshape(n_blk, 1, per)
    pos = jnp.pad(local, ((0, 0), (7, 0), (0, integrals.shape[1] - per))).astype(jnp.float32)
    got, sizes = exchange(partial, pos, own_rows, n_blk)
    return arrange(got, sizes, sizes[:, 7, :per].astype(jnp.int32).reshape(own_rows))


def solution(mesh):
    in_specs = (
        P(("tgt", "blk"), None, None),
        P("tgt", None, None),
        P(("tgt", "blk")),
        P(("tgt", "blk")),
        P(("tgt", "blk")),
        P(("tgt", "blk"), None),
        P("blk"),
    )
    out_specs = P(("tgt", "blk"), None, None)
    return jax.shard_map(
        on_device, mesh=mesh, in_specs=in_specs, out_specs=out_specs, check_vma=False
    )
```

```python
import jax
import jax.numpy as jnp
from jax import lax
from jax.experimental import pallas as pl
from jax.experimental.pallas import tpu as pltpu
from jax.sharding import PartitionSpec as P

CHUNK = 4
UNROLL = 16
STEPS = 8
LAG = 1
MESH = pl.DeviceIdType.MESH


def bits_for(n):
    return max(1, (n - 1).bit_length())


def accumulate(n_steps, keys, place, integrals, pieces, groups, st_bits, blk_bits, hb_rows):
    s_group, size, _ = pieces[0].shape
    states = s_group * len(pieces)
    st_mask = (1 << st_bits) - 1
    blk_mask = (1 << blk_bits) - 1

    def kernel(n_ref, keys_ref, place_ref, groups_ref, int_hbm, *rest):
        den_refs, (acc, ints, dens, sems) = rest[:len(pieces)], rest[len(pieces):]
        loads = [
            pltpu.make_async_copy(
                ref, dens.at[pl.ds(groups_ref[i] * s_group, s_group)], sems.at[i]
            )
            for i, ref in enumerate(den_refs)
        ]
        loads.append(pltpu.make_async_copy(int_hbm, ints, sems.at[len(pieces)]))
        for load in loads:
            load.start()
        dens[states] = jnp.zeros((size, size), dens.dtype)

        @pl.loop(0, hb_rows)
        def _(j):
            acc[j] = jnp.zeros((size, size), jnp.float32)

        for load in loads:
            load.wait()

        @pl.loop(0, n_ref[0])
        def _(step):
            prods = []
            for u in range(UNROLL):
                base = (step * UNROLL + u) * CHUNK
                ks = [keys_ref[base + i] for i in range(CHUNK)]
                lhs = jnp.concatenate([ints[(k >> st_bits) & blk_mask] for k in ks], axis=1)
                rhs = jnp.concatenate([dens[k & st_mask] for k in ks], axis=0)
                row = place_ref[ks[0] >> (st_bits + blk_bits)]
                prods.append((row, jnp.dot(lhs, rhs, preferred_element_type=jnp.float32)))
            for row, prod in prods:
                acc[row] += prod

    smem = pl.BlockSpec(memory_space=pltpu.SMEM)
    vmem = pl.BlockSpec(memory_space=pltpu.VMEM)
    hbm = pl.BlockSpec(memory_space=pl.ANY)
    return pl.pallas_call(
        kernel,
        out_shape=jax.ShapeDtypeStruct((hb_rows, size, size), jnp.float32),
        in_specs=[smem] * 4 + [hbm] * (1 + len(pieces)),
        out_specs=vmem,
        scratch_shapes=[
            pltpu.VMEM(integrals.shape, integrals.dtype),
            pltpu.VMEM((states + 1, size, size), pieces[0].dtype),
            pltpu.SemaphoreType.DMA((len(pieces) + 1,)),
        ],
        compiler_params=pltpu.CompilerParams(vmem_limit_bytes=40 << 20),
    )(n_steps, keys, place, groups, integrals, *pieces)


def make_keys(entry_block, entry_state, entry_slot, live, hb_rows, held, states):
    st_bits = bits_for(states + 1)
    blk_bits = bits_for(held)
    e_cap = entry_block.shape[0]
    valid = jnp.arange(e_cap, dtype=jnp.int32) < live
    slots = jnp.arange(hb_rows, dtype=jnp.int32)
    per_slot = jnp.sum(
        ((entry_slot[:, None] == slots[None, :]) & valid[:, None]).astype(jnp.int32), axis=0
    )
    spare = (-per_slot) % CHUNK
    filler = (slots << (st_bits + blk_bits)) + ((held - 1) << st_bits) + states
    last = filler[hb_rows - 1]
    key = (((entry_slot << blk_bits) + entry_block) << st_bits) + entry_state
    key = jnp.where(valid, key, last)
    order = jnp.arange(CHUNK - 1, dtype=jnp.int32)
    fill = jnp.where(order[:, None] < spare[None, :], filler[None, :], last).reshape(-1)
    total = e_cap + fill.shape[0]
    group = CHUNK * UNROLL
    tail = jnp.full(((-total) % group,), last, jnp.int32)
    keys = lax.sort(jnp.concatenate([key, fill, tail]), is_stable=False)
    n_steps = (jnp.sum(per_slot + spare) + group - 1) // group
    return keys, n_steps.reshape(1), st_bits, blk_bits


LEVELS = 32767.0
SMALLEST = 1e-33


def narrow(x):
    top = jnp.maximum(jnp.max(jnp.abs(x), axis=0, keepdims=True), SMALLEST)
    return jnp.round(x * (LEVELS / top)).astype(jnp.int32).astype(jnp.int16), top * (1.0 / LEVELS)


def widen(q, step):
    return q.astype(jnp.int32).astype(jnp.float32) * step


def exchange(partial, pos, own_rows, n_blk):
    size = partial.shape[-1]
    steps = min(STEPS, n_blk)
    rows = own_rows // steps
    dests = n_blk // steps
    per = own_rows // n_blk

    def kernel(part, pos_ref, out, step_out, r1, s2, r2, s3, step2, step2_in, step3,
               s1_send, s1_recv, s2_send, s2_recv, t2_send, t2_recv, s3_send, s3_recv,
               t3_send, t3_recv, own_sem):
        t = lax.axis_index("tgt")
        b = lax.axis_index("blk")
        y, c = t // 2, t % 2
        sibling = y * 2 + (1 - c)
        across = (1 - y) * 2 + c
        barrier = pltpu.get_barrier_semaphore()
        pl.semaphore_signal(barrier, inc=1, device_id={"tgt": sibling}, device_id_type=MESH)
        pl.semaphore_signal(barrier, inc=1, device_id={"tgt": across}, device_id_type=MESH)
        for i in range(1, n_blk):
            pl.semaphore_signal(
                barrier, inc=1, device_id={"blk": (b + i) % n_blk}, device_id_type=MESH
            )
        pl.semaphore_wait(barrier, n_blk + 1)

        def span(i):
            return ((b // dests + 1 + i) % steps) * rows

        def first(i, far):
            side = 1 - y if far else y
            return pltpu.make_async_remote_copy(
                src_ref=part.at[pl.ds((side * 2 + 1 - c) * own_rows + span(i), rows)],
                dst_ref=r1.at[far, pl.ds(span(i), rows)],
                send_sem=s1_send.at[far, i],
                recv_sem=s1_recv.at[far, i],
                device_id={"tgt": sibling},
                device_id_type=MESH,
            )

        def second(i):
            return pltpu.make_async_remote_copy(
                src_ref=s2.at[pl.ds(span(i), rows)],
                dst_ref=r2.at[pl.ds(span(i), rows)],
                send_sem=s2_send.at[i],
                recv_sem=s2_recv.at[i],
                device_id={"tgt": across},
                device_id_type=MESH,
            )

        def second_steps(i):
            return pltpu.make_async_remote_copy(
                src_ref=step2.at[i],
                dst_ref=step2_in.at[i],
                send_sem=t2_send.at[i],
                recv_sem=t2_recv.at[i],
                device_id={"tgt": across},
                device_id_type=MESH,
            )

        def third(dest, slot):
            return pltpu.make_async_remote_copy(
                src_ref=s3.at[pl.ds(dest * per, per)],
                dst_ref=out.at[pl.ds(slot * per, per)],
                send_sem=s3_send.at[dest],
                recv_sem=s3_recv.at[slot],
                device_id={"blk": dest},
                device_id_type=MESH,
            )

        def third_steps(dest, slot):
            return pltpu.make_async_remote_copy(
                src_ref=step3.at[dest],
                dst_ref=step_out.at[slot],
                send_sem=t3_send.at[dest],
                recv_sem=t3_recv.at[slot],
                device_id={"blk": dest},
                device_id_type=MESH,
            )

        own_out = pltpu.make_async_copy(
            s3.at[pl.ds(b * per, per)], out.at[pl.ds(b * per, per)], own_sem.at[0]
        )
        own_steps = pltpu.make_async_copy(step3.at[b], step_out.at[b], own_sem.at[1])

        for i in range(steps):
            first(i, 1).start()

        def finish(i):
            first(i, 0).wait_recv()
            second(i).wait_recv()
            second_steps(i).wait_recv()
            steps_in = step2_in[i]
            for j in range(dests):
                dest = ((b // dests + 1 + i) % steps) * dests + (b % dests + j) % dests
                step3[dest] = pos_ref[dest]
                for k in range(per):
                    row = dest * per + k
                    at = ((b % dests + j) % dests) * per + k if dests > 1 else k
                    if dests > 1:
                        scale = step2_in[i, pl.ds(at, 1), :]
                    else:
                        scale = steps_in[k:k + 1]
                    total = part[(y * 2 + c) * own_rows + row] + r1[0, row] + widen(r2[row], scale)
                    q, step = narrow(total)
                    s3[row] = q
                    step3[dest, k:k + 1, :] = step
                if i == steps - 1 and j == 0:
                    own_out.start()
                    own_steps.start()
                else:
                    third(dest, b).start()
                    third_steps(dest, b).start()

        for i in range(steps):
            first(i, 0).start()
            first(i, 1).wait_recv()
            for k in range(rows):
                row = span(i) + k
                q, step = narrow(part[((1 - y) * 2 + c) * own_rows + row] + r1[1, row])
                s2[row] = q
                step2[i, k:k + 1, :] = step
            for k in range(rows, 8):
                step2[i, k:k + 1, :] = jnp.zeros((1, size), jnp.float32)
            second(i).start()
            second_steps(i).start()
            if i >= LAG:
                finish(i - LAG)
        for i in range(max(0, steps - LAG), steps):
            finish(i)

        for i in range(steps):
            first(i, 1).wait_send()
            first(i, 0).wait_send()
            second(i).wait_send()
            second_steps(i).wait_send()
        for i in range(1, n_blk):
            peer = (b + i) % n_blk
            third(peer, b).wait_send()
            third_steps(peer, b).wait_send()
            third(peer, peer).wait_recv()
            third_steps(peer, peer).wait_recv()
        own_steps.wait()
        own_out.wait()

    vmem = pl.BlockSpec(memory_space=pltpu.VMEM)
    dma = pltpu.SemaphoreType.DMA
    block = (own_rows, size, size)
    return pl.pallas_call(
        kernel,
        out_shape=(
            jax.ShapeDtypeStruct(block, jnp.int16),
            jax.ShapeDtypeStruct(pos.shape, jnp.float32),
        ),
        in_specs=[vmem, vmem],
        out_specs=(pl.BlockSpec(memory_space=pltpu.HBM),) * 2,
        scratch_shapes=[
            pltpu.VMEM((2,) + block, jnp.float32),
            pltpu.VMEM(block, jnp.int16),
            pltpu.VMEM(block, jnp.int16),
            pltpu.VMEM(block, jnp.int16),
            pltpu.VMEM((steps, 8, size), jnp.float32),
            pltpu.VMEM((steps, 8, size), jnp.float32),
            pltpu.VMEM((n_blk, 8, size), jnp.float32),
            dma((2, steps)), dma((2, steps)),
            dma((steps,)), dma((steps,)),
            dma((steps,)), dma((steps,)),
            dma((n_blk,)), dma((n_blk,)),
            dma((n_blk,)), dma((n_blk,)),
            dma((2,)),
        ],
        compiler_params=pltpu.CompilerParams(
            collective_id=0, has_side_effects=True, vmem_limit_bytes=40 << 20
        ),
    )(partial, pos)


def arrange(blocks, sizes, target):
    n, size, _ = blocks.shape
    n_blk = sizes.shape[0]
    per = n // n_blk

    def kernel(target_ref, src, sizes_ref, dst, wide, sem):
        @pl.loop(0, n_blk)
        def _(s):
            for k in range(per):
                r = s * per + k
                wide[r] = widen(src[r], sizes_ref[s, k:k + 1, :])
                pltpu.make_async_copy(wide.at[r], dst.at[target_ref[r]], sem).start()

        pltpu.make_async_copy(wide, dst, sem).wait()

    vmem = pl.BlockSpec(memory_space=pltpu.VMEM)
    return pl.pallas_call(
        kernel,
        out_shape=jax.ShapeDtypeStruct(blocks.shape, jnp.float32),
        in_specs=[pl.BlockSpec(memory_space=pltpu.SMEM), vmem, vmem],
        out_specs=pl.BlockSpec(memory_space=pl.ANY),
        scratch_shapes=[pltpu.VMEM(blocks.shape, jnp.float32), pltpu.SemaphoreType.DMA],
    )(target, blocks, sizes)


def on_device(integrals, densities, entry_block, entry_state, entry_slot, counts, owner):
    hb_rows = owner.shape[0]
    n_tgt = lax.axis_size("tgt")
    n_blk = lax.axis_size("blk")
    own_rows = hb_rows // n_tgt
    per = own_rows // n_blk
    t = lax.axis_index("tgt")
    over = [(i, i ^ 2) for i in range(n_tgt)]
    beside = [(i, i ^ 1) for i in range(n_tgt)]
    far = lax.ppermute(densities, "tgt", over)
    near = lax.ppermute(densities, "tgt", beside)
    far_near = lax.ppermute(far, "tgt", beside)
    pieces = (densities, near, far, far_near)
    groups = t ^ jnp.arange(4, dtype=jnp.int32)
    keys, n_steps, st_bits, blk_bits = make_keys(
        entry_block, entry_state, entry_slot, jnp.sum(counts[0]), hb_rows,
        integrals.shape[0], densities.shape[0] * n_tgt,
    )
    place = jnp.sum((owner[None, :] < owner[:, None]).astype(jnp.int32), axis=1)
    partial = accumulate(
        n_steps, keys, place, integrals, pieces, groups, st_bits, blk_bits, hb_rows
    )
    ranks = t * own_rows + jnp.arange(own_rows, dtype=jnp.int32)
    hit = (place[None, :] == ranks[:, None]).astype(jnp.int32)
    local = jnp.sum(hit * (owner % own_rows)[None, :], axis=1).reshape(n_blk, 1, per)
    pos = jnp.pad(local, ((0, 0), (7, 0), (0, integrals.shape[1] - per))).astype(jnp.float32)
    got, sizes = exchange(partial, pos, own_rows, n_blk)
    return arrange(got, sizes, sizes[:, 7, :per].astype(jnp.int32).reshape(own_rows))


def solution(mesh):
    in_specs = (
        P(("tgt", "blk"), None, None),
        P("tgt", None, None),
        P(("tgt", "blk")),
        P(("tgt", "blk")),
        P(("tgt", "blk")),
        P(("tgt", "blk"), None),
        P("blk"),
    )
    out_specs = P(("tgt", "blk"), None, None)
    return jax.shard_map(
        on_device, mesh=mesh, in_specs=in_specs, out_specs=out_specs, check_vma=False
    )
```

```python
import jax
import jax.numpy as jnp
from jax import lax
from jax.experimental import pallas as pl
from jax.experimental.pallas import tpu as pltpu
from jax.sharding import PartitionSpec as P

CHUNK = 4
UNROLL = 16
STEPS = 8
LAG = 2
MESH = pl.DeviceIdType.MESH


def bits_for(n):
    return max(1, (n - 1).bit_length())


def accumulate(n_steps, keys, place, integrals, pieces, groups, st_bits, blk_bits, hb_rows):
    s_group, size, _ = pieces[0].shape
    states = s_group * len(pieces)
    st_mask = (1 << st_bits) - 1
    blk_mask = (1 << blk_bits) - 1

    def kernel(n_ref, keys_ref, place_ref, groups_ref, int_hbm, *rest):
        den_refs, (acc, ints, dens, sems) = rest[:len(pieces)], rest[len(pieces):]
        loads = [
            pltpu.make_async_copy(
                ref, dens.at[pl.ds(groups_ref[i] * s_group, s_group)], sems.at[i]
            )
            for i, ref in enumerate(den_refs)
        ]
        loads.append(pltpu.make_async_copy(int_hbm, ints, sems.at[len(pieces)]))
        for load in loads:
            load.start()
        dens[states] = jnp.zeros((size, size), dens.dtype)

        @pl.loop(0, hb_rows)
        def _(j):
            acc[j] = jnp.zeros((size, size), jnp.float32)

        for load in loads:
            load.wait()

        @pl.loop(0, n_ref[0])
        def _(step):
            prods = []
            for u in range(UNROLL):
                base = (step * UNROLL + u) * CHUNK
                ks = [keys_ref[base + i] for i in range(CHUNK)]
                lhs = jnp.concatenate([ints[(k >> st_bits) & blk_mask] for k in ks], axis=1)
                rhs = jnp.concatenate([dens[k & st_mask] for k in ks], axis=0)
                row = place_ref[ks[0] >> (st_bits + blk_bits)]
                prods.append((row, jnp.dot(lhs, rhs, preferred_element_type=jnp.float32)))
            for row, prod in prods:
                acc[row] += prod

    smem = pl.BlockSpec(memory_space=pltpu.SMEM)
    vmem = pl.BlockSpec(memory_space=pltpu.VMEM)
    hbm = pl.BlockSpec(memory_space=pl.ANY)
    return pl.pallas_call(
        kernel,
        out_shape=jax.ShapeDtypeStruct((hb_rows, size, size), jnp.float32),
        in_specs=[smem] * 4 + [hbm] * (1 + len(pieces)),
        out_specs=vmem,
        scratch_shapes=[
            pltpu.VMEM(integrals.shape, integrals.dtype),
            pltpu.VMEM((states + 1, size, size), pieces[0].dtype),
            pltpu.SemaphoreType.DMA((len(pieces) + 1,)),
        ],
        compiler_params=pltpu.CompilerParams(vmem_limit_bytes=40 << 20),
    )(n_steps, keys, place, groups, integrals, *pieces)


def make_keys(entry_block, entry_state, entry_slot, live, hb_rows, held, states):
    st_bits = bits_for(states + 1)
    blk_bits = bits_for(held)
    e_cap = entry_block.shape[0]
    valid = jnp.arange(e_cap, dtype=jnp.int32) < live
    slots = jnp.arange(hb_rows, dtype=jnp.int32)
    per_slot = jnp.sum(
        ((entry_slot[:, None] == slots[None, :]) & valid[:, None]).astype(jnp.int32), axis=0
    )
    spare = (-per_slot) % CHUNK
    filler = (slots << (st_bits + blk_bits)) + ((held - 1) << st_bits) + states
    last = filler[hb_rows - 1]
    key = (((entry_slot << blk_bits) + entry_block) << st_bits) + entry_state
    key = jnp.where(valid, key, last)
    order = jnp.arange(CHUNK - 1, dtype=jnp.int32)
    fill = jnp.where(order[:, None] < spare[None, :], filler[None, :], last).reshape(-1)
    total = e_cap + fill.shape[0]
    group = CHUNK * UNROLL
    tail = jnp.full(((-total) % group,), last, jnp.int32)
    keys = lax.sort(jnp.concatenate([key, fill, tail]), is_stable=False)
    n_steps = (jnp.sum(per_slot + spare) + group - 1) // group
    return keys, n_steps.reshape(1), st_bits, blk_bits


LEVELS = 32767.0
SMALLEST = 1e-33


def narrow(x):
    top = jnp.maximum(jnp.max(jnp.abs(x), axis=0, keepdims=True), SMALLEST)
    return jnp.round(x * (LEVELS / top)).astype(jnp.int32).astype(jnp.int16), top * (1.0 / LEVELS)


def widen(q, step):
    return q.astype(jnp.int32).astype(jnp.float32) * step


def exchange(partial, pos, own_rows, n_blk):
    size = partial.shape[-1]
    steps = min(STEPS, n_blk)
    rows = own_rows // steps
    dests = n_blk // steps
    per = own_rows // n_blk

    def kernel(part, pos_ref, out, step_out, r1, s2, r2, s3, step2, step2_in, step3,
               s1_send, s1_recv, s2_send, s2_recv, t2_send, t2_recv, s3_send, s3_recv,
               t3_send, t3_recv, own_sem):
        t = lax.axis_index("tgt")
        b = lax.axis_index("blk")
        y, c = t // 2, t % 2
        sibling = y * 2 + (1 - c)
        across = (1 - y) * 2 + c
        barrier = pltpu.get_barrier_semaphore()
        pl.semaphore_signal(barrier, inc=1, device_id={"tgt": sibling}, device_id_type=MESH)
        pl.semaphore_signal(barrier, inc=1, device_id={"tgt": across}, device_id_type=MESH)
        for i in range(1, n_blk):
            pl.semaphore_signal(
                barrier, inc=1, device_id={"blk": (b + i) % n_blk}, device_id_type=MESH
            )
        pl.semaphore_wait(barrier, n_blk + 1)

        def span(i):
            return ((b // dests + 1 + i) % steps) * rows

        def first(i, far):
            side = 1 - y if far else y
            return pltpu.make_async_remote_copy(
                src_ref=part.at[pl.ds((side * 2 + 1 - c) * own_rows + span(i), rows)],
                dst_ref=r1.at[far, pl.ds(span(i), rows)],
                send_sem=s1_send.at[far, i],
                recv_sem=s1_recv.at[far, i],
                device_id={"tgt": sibling},
                device_id_type=MESH,
            )

        def second(i):
            return pltpu.make_async_remote_copy(
                src_ref=s2.at[pl.ds(span(i), rows)],
                dst_ref=r2.at[pl.ds(span(i), rows)],
                send_sem=s2_send.at[i],
                recv_sem=s2_recv.at[i],
                device_id={"tgt": across},
                device_id_type=MESH,
            )

        def second_steps(i):
            return pltpu.make_async_remote_copy(
                src_ref=step2.at[i],
                dst_ref=step2_in.at[i],
                send_sem=t2_send.at[i],
                recv_sem=t2_recv.at[i],
                device_id={"tgt": across},
                device_id_type=MESH,
            )

        def third(dest, slot):
            return pltpu.make_async_remote_copy(
                src_ref=s3.at[pl.ds(dest * per, per)],
                dst_ref=out.at[pl.ds(slot * per, per)],
                send_sem=s3_send.at[dest],
                recv_sem=s3_recv.at[slot],
                device_id={"blk": dest},
                device_id_type=MESH,
            )

        def third_steps(dest, slot):
            return pltpu.make_async_remote_copy(
                src_ref=step3.at[dest],
                dst_ref=step_out.at[slot],
                send_sem=t3_send.at[dest],
                recv_sem=t3_recv.at[slot],
                device_id={"blk": dest},
                device_id_type=MESH,
            )

        own_out = pltpu.make_async_copy(
            s3.at[pl.ds(b * per, per)], out.at[pl.ds(b * per, per)], own_sem.at[0]
        )
        own_steps = pltpu.make_async_copy(step3.at[b], step_out.at[b], own_sem.at[1])

        for i in range(steps):
            first(i, 1).start()

        def finish(i):
            first(i, 0).wait_recv()
            second(i).wait_recv()
            second_steps(i).wait_recv()
            steps_in = step2_in[i]
            for j in range(dests):
                dest = ((b // dests + 1 + i) % steps) * dests + (b % dests + j) % dests
                step3[dest] = pos_ref[dest]
                for k in range(per):
                    row = dest * per + k
                    at = ((b % dests + j) % dests) * per + k if dests > 1 else k
                    if dests > 1:
                        scale = step2_in[i, pl.ds(at, 1), :]
                    else:
                        scale = steps_in[k:k + 1]
                    total = part[(y * 2 + c) * own_rows + row] + r1[0, row] + widen(r2[row], scale)
                    q, step = narrow(total)
                    s3[row] = q
                    step3[dest, k:k + 1, :] = step
                if i == steps - 1 and j == 0:
                    own_out.start()
                    own_steps.start()
                else:
                    third(dest, b).start()
                    third_steps(dest, b).start()

        for i in range(steps):
            first(i, 0).start()
            first(i, 1).wait_recv()
            for k in range(rows):
                row = span(i) + k
                q, step = narrow(part[((1 - y) * 2 + c) * own_rows + row] + r1[1, row])
                s2[row] = q
                step2[i, k:k + 1, :] = step
            for k in range(rows, 8):
                step2[i, k:k + 1, :] = jnp.zeros((1, size), jnp.float32)
            second(i).start()
            second_steps(i).start()
            if i >= LAG:
                finish(i - LAG)
        for i in range(max(0, steps - LAG), steps):
            finish(i)

        for i in range(steps):
            first(i, 1).wait_send()
            first(i, 0).wait_send()
            second(i).wait_send()
            second_steps(i).wait_send()
        for i in range(1, n_blk):
            peer = (b + i) % n_blk
            third(peer, b).wait_send()
            third_steps(peer, b).wait_send()
            third(peer, peer).wait_recv()
            third_steps(peer, peer).wait_recv()
        own_steps.wait()
        own_out.wait()

    vmem = pl.BlockSpec(memory_space=pltpu.VMEM)
    dma = pltpu.SemaphoreType.DMA
    block = (own_rows, size, size)
    return pl.pallas_call(
        kernel,
        out_shape=(
            jax.ShapeDtypeStruct(block, jnp.int16),
            jax.ShapeDtypeStruct(pos.shape, jnp.float32),
        ),
        in_specs=[vmem, vmem],
        out_specs=(pl.BlockSpec(memory_space=pltpu.HBM),) * 2,
        scratch_shapes=[
            pltpu.VMEM((2,) + block, jnp.float32),
            pltpu.VMEM(block, jnp.int16),
            pltpu.VMEM(block, jnp.int16),
            pltpu.VMEM(block, jnp.int16),
            pltpu.VMEM((steps, 8, size), jnp.float32),
            pltpu.VMEM((steps, 8, size), jnp.float32),
            pltpu.VMEM((n_blk, 8, size), jnp.float32),
            dma((2, steps)), dma((2, steps)),
            dma((steps,)), dma((steps,)),
            dma((steps,)), dma((steps,)),
            dma((n_blk,)), dma((n_blk,)),
            dma((n_blk,)), dma((n_blk,)),
            dma((2,)),
        ],
        compiler_params=pltpu.CompilerParams(
            collective_id=0, has_side_effects=True, vmem_limit_bytes=40 << 20
        ),
    )(partial, pos)


def arrange(blocks, sizes, target):
    n, size, _ = blocks.shape
    n_blk = sizes.shape[0]
    per = n // n_blk

    def kernel(target_ref, src, sizes_ref, dst, wide, sem):
        @pl.loop(0, n_blk)
        def _(s):
            for k in range(per):
                r = s * per + k
                wide[r] = widen(src[r], sizes_ref[s, k:k + 1, :])
                pltpu.make_async_copy(wide.at[r], dst.at[target_ref[r]], sem).start()

        pltpu.make_async_copy(wide, dst, sem).wait()

    vmem = pl.BlockSpec(memory_space=pltpu.VMEM)
    return pl.pallas_call(
        kernel,
        out_shape=jax.ShapeDtypeStruct(blocks.shape, jnp.float32),
        in_specs=[pl.BlockSpec(memory_space=pltpu.SMEM), vmem, vmem],
        out_specs=pl.BlockSpec(memory_space=pl.ANY),
        scratch_shapes=[pltpu.VMEM(blocks.shape, jnp.float32), pltpu.SemaphoreType.DMA],
    )(target, blocks, sizes)


def on_device(integrals, densities, entry_block, entry_state, entry_slot, counts, owner):
    hb_rows = owner.shape[0]
    n_tgt = lax.axis_size("tgt")
    n_blk = lax.axis_size("blk")
    own_rows = hb_rows // n_tgt
    per = own_rows // n_blk
    t = lax.axis_index("tgt")
    over = [(i, i ^ 2) for i in range(n_tgt)]
    beside = [(i, i ^ 1) for i in range(n_tgt)]
    far = lax.ppermute(densities, "tgt", over)
    near = lax.ppermute(densities, "tgt", beside)
    far_near = lax.ppermute(far, "tgt", beside)
    pieces = (densities, near, far, far_near)
    groups = t ^ jnp.arange(4, dtype=jnp.int32)
    keys, n_steps, st_bits, blk_bits = make_keys(
        entry_block, entry_state, entry_slot, jnp.sum(counts[0]), hb_rows,
        integrals.shape[0], densities.shape[0] * n_tgt,
    )
    place = jnp.sum((owner[None, :] < owner[:, None]).astype(jnp.int32), axis=1)
    partial = accumulate(
        n_steps, keys, place, integrals, pieces, groups, st_bits, blk_bits, hb_rows
    )
    ranks = t * own_rows + jnp.arange(own_rows, dtype=jnp.int32)
    hit = (place[None, :] == ranks[:, None]).astype(jnp.int32)
    local = jnp.sum(hit * (owner % own_rows)[None, :], axis=1).reshape(n_blk, 1, per)
    pos = jnp.pad(local, ((0, 0), (7, 0), (0, integrals.shape[1] - per))).astype(jnp.float32)
    got, sizes = exchange(partial, pos, own_rows, n_blk)
    return arrange(got, sizes, sizes[:, 7, :per].astype(jnp.int32).reshape(own_rows))


def solution(mesh):
    in_specs = (
        P(("tgt", "blk"), None, None),
        P("tgt", None, None),
        P(("tgt", "blk")),
        P(("tgt", "blk")),
        P(("tgt", "blk")),
        P(("tgt", "blk"), None),
        P("blk"),
    )
    out_specs = P(("tgt", "blk"), None, None)
    return jax.shard_map(
        on_device, mesh=mesh, in_specs=in_specs, out_specs=out_specs, check_vma=False
    )
```
